32 devices in a mesh: grid: 2 (over x), row: 4 (over y, core), col: 4 (over z).
Axes of the slice: x: 2, y: 2, z: 4, core: 2. Of those that a mesh axis runs over, the one named last changes fastest.
Arguments:
- rhs_in: bfloat16 [32768, 1024], P(('grid', 'row', 'col')), may hold values from -6 to 6
- rhs_target: int32 [32768], P(('grid', 'row', 'col')), may hold values from 0 to 32767, as said below
- leaf_inverse: bfloat16 [64, 512, 512], P(('grid', 'row', 'col')), may hold values from -0.25 to 0.25
- level_one_blocks: bfloat16 [2, 4, 4, 4, 2, 512, 512], P('grid', 'row', 'col'), may hold values from -0.0625 to 0.0625
- level_one_pattern: int32 [2, 4, 4, 4, 2], P('grid', 'row', 'col'), may hold values 0 or 1
- level_one_rhs: bfloat16 [2, 4, 512, 1024], P('grid', 'row', None, 'col'), may hold values from -6 to 6
- level_one_inverse: bfloat16 [2, 4, 512, 512], P('grid', 'row'), may hold values from -0.25 to 0.25
- top_blocks: bfloat16 [2, 4, 4, 512, 512], P('grid', 'row'), may hold values from -0.09375 to 0.09375
- top_rhs: bfloat16 [4, 512, 1024], P(None, None, 'col'), may hold values from -6 to 6
- top_inverse: bfloat16 [4, 512, 512], replicated, may hold values from -0.25 to 0.25
- top_chain: bfloat16 [6, 512, 512], replicated, may hold values from -0.125 to 0.125
Outputs:
- leaf_solution: bfloat16 [32768, 1024], P(('grid', 'row', 'col'))
- level_one_solution: bfloat16 [2, 4, 512, 1024], P('grid', 'row', None, 'col')
- top_solution: bfloat16 [4, 512, 1024], P(None, None, 'col')
The draws below stay inside these ranges and needn't reach their ends.
Inputs may be any that keep to these rules, and one draw needn't show every extreme that they name: rhs_target is a permutation; position p belongs to the device of flat index p // 1024 over grid, row, col (grid slowest); the 1024 arrival rows of every device go exactly 32 to each device.
All inputs are finite; a program needn't handle non-finite values. No bound on the sum of `level_one_pattern` on one device may be relied on, other than what follows from the above.
Results may differ from the reference program's by a relative error of at most 0.02.
Values may be sent and summed in bfloat16 or wider, within the bound.
A program may use at most 128 MiB of HBM per device.

```python
import jax
import jax.numpy as jnp
from jax import lax

S = 512
R = 1024
LEAF_DEV = 2
TOPS = 4
GRIDS = 2
BROWS = 4
BCOLS = 4
ROWS_DEV = 1024
ALL_ROWS = 32768
LEAVES = 64
PAIRS = 6


def draw_rhs_target(key, part):
    device_count = ALL_ROWS // ROWS_DEV
    share_rows = ROWS_DEV // device_count
    first_key, second_key = jax.random.split(jax.random.fold_in(key, 17))
    column_ids = jnp.arange(ROWS_DEV, dtype=jnp.int32)[None, :]
    scores = jax.random.randint(first_key, (device_count, ROWS_DEV), 0, 65536) * ROWS_DEV + column_ids
    local_order = jnp.argsort(scores, axis=1).astype(jnp.int32)
    grouped = local_order.reshape(device_count, device_count, share_rows)
    owners = jnp.arange(device_count, dtype=jnp.int32)[:, None, None] * ROWS_DEV
    positions = grouped + owners
    per_source = jnp.transpose(positions, (1, 0, 2)).reshape(device_count, ROWS_DEV)
    shuffle_scores = jax.random.randint(second_key, (device_count, ROWS_DEV), 0, 65536) * ROWS_DEV + column_ids
    shuffle = jnp.argsort(shuffle_scores, axis=1)
    mixed = jnp.take_along_axis(per_source, shuffle, axis=1)
    return mixed.reshape(ALL_ROWS).astype(jnp.int32)


def set_ends(array, rng, low, high):
    place = [jax.random.randint(jax.random.fold_in(rng, axis), (), 0, length) for axis, length in enumerate(array.shape)]
    main_axis = array.shape.index(max(array.shape))
    next_to = place[:main_axis] + [(place[main_axis] + 1) % array.shape[main_axis]] + place[main_axis + 1:]
    return array.at[tuple(place)].set(low).at[tuple(next_to)].set(high)


def block_levels(own_key, extent, cuts, least, top_value):
    def one(axis_at, shards_of):
        steps = jax.random.uniform(jax.random.fold_in(jax.random.fold_in(own_key, 6), axis_at), (shards_of,), jnp.float32, least / len(cuts), top_value / len(cuts))
        return jnp.repeat(jnp.exp(steps), extent[axis_at] // shards_of).reshape((-1,) + (1,) * (len(extent) - axis_at - 1))

    level = one(*cuts[0])
    for cut in cuts[1:]:
        level = level * one(*cut)
    return level


def bell_draw(stream_key, extent, scale, limit, cuts=(), held_as=jnp.bfloat16):
    factor_of = block_levels(stream_key, extent, cuts, -0.22, 0.18) if cuts else 1.0
    array = jax.random.normal(stream_key, extent, jnp.float32) * scale * factor_of
    return jnp.minimum(jnp.maximum(array, -limit), limit).astype(held_as)


def setup_inputs(seed: int = 0) -> dict:
    splits = jax.random.split(jax.random.key(seed), 12)
    rhs_in = bell_draw(splits[0], (ALL_ROWS, R), 1.0, 6.0, ((0, 32),))
    rhs_target = draw_rhs_target(jax.random.fold_in(splits[11], 71), 0)
    leaf_inverse = bell_draw(splits[2], (LEAVES, S, S), S ** -0.5, 0.25, ((0, 32),))
    level_one_blocks = bell_draw(splits[3], (GRIDS, BROWS, BCOLS, BROWS, LEAF_DEV, S, S), (BROWS * BCOLS * LEAF_DEV * S // 2) ** -0.5, 0.0625, ((0, 2), (1, 4), (2, 4)))
    level_one_pattern = set_ends((jax.random.randint(splits[4], (GRIDS, BROWS, BCOLS, BROWS, LEAF_DEV), 0, 2) < 1).astype(jnp.int32), jax.random.fold_in(splits[4], 1), 0, 1)
    level_one_rhs = bell_draw(splits[5], (GRIDS, BROWS, S, R), 1.0, 6.0, ((0, 2), (1, 4), (3, 4)))
    level_one_inverse = bell_draw(splits[6], (GRIDS, BROWS, S, S), S ** -0.5, 0.25, ((0, 2), (1, 4)))
    top_blocks = bell_draw(splits[7], (GRIDS, BROWS, TOPS, S, S), (GRIDS * BROWS * S) ** -0.5, 0.09375, ((0, 2), (1, 4)))
    top_rhs = bell_draw(splits[8], (TOPS, S, R), 1.0, 6.0, ((2, 4),))
    top_inverse = bell_draw(splits[9], (TOPS, S, S), S ** -0.5, 0.25)
    top_chain = bell_draw(splits[10], (PAIRS, S, S), (TOPS * S) ** -0.5, 0.125)
    return {"rhs_in": rhs_in, "rhs_target": rhs_target, "leaf_inverse": leaf_inverse, "level_one_blocks": level_one_blocks, "level_one_pattern": level_one_pattern, "level_one_rhs": level_one_rhs, "level_one_inverse": level_one_inverse, "top_blocks": top_blocks, "top_rhs": top_rhs, "top_inverse": top_inverse, "top_chain": top_chain}


def leaf_solve(operands):
    inverse_block, rhs_block = operands
    return jnp.dot(inverse_block, rhs_block, preferred_element_type=jnp.float32).astype(jnp.bfloat16)


def level_one_grid(operands):
    leaf_grid, blocks, pattern, rhs_one, inverse_one = operands
    solved = leaf_grid.astype(jnp.float32)
    masked = blocks.astype(jnp.float32) * pattern.astype(jnp.float32)[..., None, None]
    update_one = jnp.einsum("kcmlij,mcljr->kir", masked, solved)
    resid_one = (rhs_one.astype(jnp.float32) - update_one).astype(jnp.bfloat16)
    return jnp.einsum("kij,kjr->kir", inverse_one.astype(jnp.float32), resid_one.astype(jnp.float32)).astype(jnp.bfloat16)


def reference(rhs_in, rhs_target, leaf_inverse, level_one_blocks, level_one_pattern, level_one_rhs, level_one_inverse, top_blocks, top_rhs, top_inverse, top_chain):
    placed = rhs_in[jnp.argsort(rhs_target)]
    leaf_rhs = placed.reshape(LEAVES, S, R)
    leaf_solution = lax.map(leaf_solve, (leaf_inverse, leaf_rhs))
    leaf_grid = leaf_solution.reshape(GRIDS, BROWS, BCOLS, LEAF_DEV, S, R)
    level_one_solution = lax.map(level_one_grid, (leaf_grid, level_one_blocks, level_one_pattern, level_one_rhs, level_one_inverse))
    top_update = jnp.einsum("gktij,gkjr->tir", top_blocks.astype(jnp.float32), level_one_solution.astype(jnp.float32))
    solved = []
    for current in range(TOPS):
        running = top_rhs[current].astype(jnp.float32) - top_update[current]
        for earlier in range(current):
            running = running - jnp.dot(top_chain[current * (current - 1) // 2 + earlier], solved[earlier], preferred_element_type=jnp.float32)
        solved.append(jnp.dot(top_inverse[current], running.astype(jnp.bfloat16), preferred_element_type=jnp.float32).astype(jnp.bfloat16))
    top_solution = jnp.stack(solved)
    return leaf_solution.reshape(ALL_ROWS, R), level_one_solution, top_solution
```

```python
import functools

import jax
import jax.numpy as jnp
from jax import lax
from jax.experimental import pallas as pl
from jax.experimental.pallas import tpu as pltpu
from jax.sharding import PartitionSpec as P

MESH = pl.DeviceIdType.MESH
VMEM = pl.BlockSpec(memory_space=pltpu.VMEM)
ANY = pl.BlockSpec(memory_space=pl.ANY)


def greet(axes, sizes):
    barrier = pltpu.get_barrier_semaphore()
    total = 1
    for size in sizes:
        total *= size
    flat = 0
    for axis, size in zip(axes, sizes):
        flat = flat * size + lax.axis_index(axis)

    @pl.loop(1, total)
    def _(step):
        rest = lax.rem(flat + step, total)
        coords = {}
        for axis, size in reversed(list(zip(axes, sizes))):
            coords[axis] = lax.rem(rest, size)
            rest = rest // size
        pl.semaphore_signal(barrier, inc=1, device_id=coords, device_id_type=MESH)

    pl.semaphore_wait(barrier, total - 1)


def dot(a, b):
    return jnp.dot(a, b, preferred_element_type=jnp.float32)


def dot_t(a, b):
    return lax.dot_general(a, b, (((1,), (1,)), ((), ())), preferred_element_type=jnp.float32)


def level_one_kernel(
    rows,
    cols,
    sol_ref,
    blocks_ref,
    pattern_ref,
    rhs_ref,
    inverse_ref,
    out_ref,
    gathered,
    other_blocks,
    other_pattern,
    totals,
    pieces,
    landed,
    block_sems,
    pattern_sems,
    gather_send,
    gather_recv,
    piece_send,
    piece_recv,
):
    me = lax.axis_index("row")
    col = lax.axis_index("col")
    side = lax.rem(me, 2)
    mate = me + 1 - 2 * side
    leaves, _, width = sol_ref.shape
    half = width // 2
    half_cols = cols // 2
    share = width // cols

    def row_at(offset):
        pair = lax.rem(me // 2 + offset // 2, rows // 2)
        return pair * 2 + lax.rem(side + offset % 2, 2)

    greet(("row", "col"), (rows, cols))

    def gather_copy(target, owner, leaf):
        begin = pl.multiple_of(lax.rem(target, 2) * half, half)
        return pltpu.make_async_remote_copy(
            src_ref=sol_ref.at[leaf, :, pl.ds(begin, half)],
            dst_ref=gathered.at[owner, leaf],
            send_sem=gather_send.at[target, leaf],
            recv_sem=gather_recv.at[owner, leaf],
            device_id={"row": target},
            device_id_type=MESH,
        )

    for leaf in range(leaves):
        for offset in range(rows - 1, 0, -1):
            if offset != 1:
                gather_copy(row_at(offset), me, leaf).start()
    pattern_copy = pltpu.make_async_remote_copy(
        src_ref=pattern_ref,
        dst_ref=other_pattern,
        send_sem=pattern_sems.at[0],
        recv_sem=pattern_sems.at[1],
        device_id={"row": mate},
        device_id_type=MESH,
    )
    pattern_copy.start()

    def block_copy(owner):
        return pltpu.make_async_remote_copy(
            src_ref=blocks_ref.at[owner],
            dst_ref=other_blocks.at[owner],
            send_sem=block_sems.at[0, owner],
            recv_sem=block_sems.at[1, owner],
            device_id={"row": mate},
            device_id_type=MESH,
        )

    block_copy(mate).start()
    for leaf in range(leaves):
        gather_copy(mate, me, leaf).start()
    for offset in range(1, rows):
        block_copy(row_at(offset - 1 if offset % 2 else offset + 1)).start()
    totals[...] = jnp.zeros_like(totals)
    mine = pl.multiple_of(side * half, half)
    for leaf in range(leaves):
        gathered[me, leaf] = sol_ref[leaf, :, pl.ds(mine, half)]

    def add(which, blocks, pattern, owner, leaf):
        block = blocks[owner, leaf]
        mask = pattern[owner, leaf]
        tall = block.shape[0] // mask.shape[0]
        masked = (block.reshape(tall, *mask.shape) * mask[None]).reshape(block.shape)
        totals[which] += dot(masked, gathered[owner, leaf])

    for leaf in range(leaves):
        add(0, blocks_ref, pattern_ref, me, leaf)
    pattern_copy.wait()

    def meet(offset):
        owner = row_at(offset)
        block_copy(owner).wait()
        for leaf in range(leaves):
            if offset:
                gather_copy(owner, owner, leaf).wait_recv()
                add(0, blocks_ref, pattern_ref, owner, leaf)
            add(1, other_blocks, other_pattern, owner, leaf)

    for offset in range(rows):
        meet(offset)
    for offset in range(1, rows):
        for leaf in range(leaves):
            gather_copy(row_at(offset), me, leaf).wait_send()

    def piece_copy(which, part):
        return pltpu.make_async_remote_copy(
            src_ref=pieces.at[which, part],
            dst_ref=landed.at[col],
            send_sem=piece_send.at[which, part],
            recv_sem=piece_recv.at[col],
            device_id={"row": mate if which else me, "col": side * half_cols + part},
            device_id_type=MESH,
        )

    for part in range(half_cols):
        for which in range(2):
            pieces[which, part] = totals[which, :, part * share : (part + 1) * share].astype(
                pieces.dtype
            )
    for part in range(half_cols):
        for which in range(2):
            stays = (side * half_cols + part == col) if which == 0 else None
            if stays is None:
                piece_copy(which, part).start()
            else:

                @pl.when(jnp.logical_not(stays))
                def _(which=which, part=part):
                    piece_copy(which, part).start()

                @pl.when(stays)
                def _(which=which, part=part):
                    landed[col] = pieces[which, part]

    source_side = col // half_cols
    for step in range(cols):
        source = lax.rem(col + step, cols)
        arrival = pltpu.make_async_remote_copy(
            src_ref=pieces.at[0, 0],
            dst_ref=landed.at[source],
            send_sem=piece_send.at[0, 0],
            recv_sem=piece_recv.at[source],
            device_id={"row": mate},
            device_id_type=MESH,
        )
        if step == 0:

            @pl.when(source_side != side)
            def _():
                arrival.wait_recv()
        else:
            arrival.wait_recv()
    for part in range(half_cols):

        @pl.when(side * half_cols + part != col)
        def _(part=part):
            piece_copy(0, part).wait_send()

        piece_copy(1, part).wait_send()
    update = landed[0].astype(jnp.float32)
    for step in range(1, cols):
        update = update + landed[step].astype(jnp.float32)
    resid = (rhs_ref[...].astype(jnp.float32) - update).astype(jnp.bfloat16)
    out_ref[...] = dot(inverse_ref[...], resid).astype(jnp.bfloat16)


def level_one(sol, blocks, pattern, rhs, inverse):
    rows, cols = lax.axis_size("row"), lax.axis_size("col")
    owners, leaves, size, _ = blocks.shape
    width = sol.shape[2]
    half, share = width // 2, width // cols
    bf16 = jnp.bfloat16
    mask = jnp.broadcast_to(pattern.astype(bf16)[:, :, None, None], (owners, leaves, 16, size))
    dma = pltpu.SemaphoreType.DMA
    return pl.pallas_call(
        functools.partial(level_one_kernel, rows, cols),
        out_shape=jax.ShapeDtypeStruct(rhs.shape, bf16),
        in_specs=[VMEM] * 5,
        out_specs=VMEM,
        scratch_shapes=[
            pltpu.VMEM((owners, leaves, size, half), bf16),
            pltpu.VMEM(blocks.shape, bf16),
            pltpu.VMEM(mask.shape, bf16),
            pltpu.VMEM((2, size, half), jnp.float32),
            pltpu.VMEM((2, cols // 2, size, share), bf16),
            pltpu.VMEM((cols, size, share), bf16),
            dma((2, owners)),
            dma((2,)),
            dma((rows, leaves)),
            dma((rows, leaves)),
            dma((2, cols // 2)),
            dma((cols,)),
        ],
        compiler_params=pltpu.CompilerParams(
            collective_id=1, has_side_effects=True, vmem_limit_bytes=48 * 2**20
        ),
        name="level_one",
    )(sol, blocks, mask, rhs, inverse)


def top_kernel(
    grids,
    rows,
    sol_ref,
    blocks_ref,
    rhs_ref,
    inverse_hbm,
    chain_hbm,
    out_ref,
    inverse_ref,
    chain_ref,
    terms,
    landed,
    load_sems,
    term_send,
    term_recv,
    out_send,
    out_recv,
):
    group = grids * rows
    me = lax.axis_index("grid") * rows + lax.axis_index("row")
    tops, size = blocks_ref.shape[0], blocks_ref.shape[1]
    depth = terms.shape[2]
    loads = (
        pltpu.make_async_copy(inverse_hbm, inverse_ref, load_sems.at[0]),
        pltpu.make_async_copy(chain_hbm, chain_ref, load_sems.at[1]),
    )
    for load in loads:
        load.start()
    greet(("grid", "row"), (grids, rows))
    turned = sol_ref[...].T

    def peer(step):
        return lax.rem(me + step, group)

    def term_copy(step, top, slot):
        target = peer(step)
        return pltpu.make_async_remote_copy(
            src_ref=terms.at[target, top],
            dst_ref=landed.at[slot, top],
            send_sem=term_send.at[target, top],
            recv_sem=term_recv.at[slot, top],
            device_id={"grid": target // rows, "row": lax.rem(target, rows)},
            device_id_type=MESH,
        )

    def out_copy(step, top, slot):
        target = peer(step)
        return pltpu.make_async_remote_copy(
            src_ref=out_ref.at[me, top],
            dst_ref=out_ref.at[slot, top],
            send_sem=out_send.at[target, top],
            recv_sem=out_recv.at[slot, top],
            device_id={"grid": target // rows, "row": lax.rem(target, rows)},
            device_id_type=MESH,
        )

    for top in range(tops):
        term = dot_t(turned, blocks_ref[top]).astype(terms.dtype)
        terms[:, top] = term.reshape(group, depth, size)

        @pl.loop(1, group)
        def _(step, top=top):
            term_copy(step, top, me).start()

    for load in loads:
        load.wait()
    for top in range(tops):

        @pl.loop(1, group)
        def _(step, top=top):
            term_copy(step, top, peer(step)).wait_recv()

        landed[me, top] = terms[me, top]
        update = landed[0, top].astype(jnp.float32)
        for other in range(1, group):
            update = update + landed[other, top].astype(jnp.float32)
        running = rhs_ref[top].astype(jnp.float32) - update
        for earlier in range(top):
            running = running - dot_t(
                out_ref[me, earlier], chain_ref[top * (top - 1) // 2 + earlier]
            )
        out_ref[me, top] = dot_t(running.astype(jnp.bfloat16), inverse_ref[top]).astype(
            jnp.bfloat16
        )

        @pl.loop(1, group)
        def _(step, top=top):
            out_copy(step, top, me).start()

    for top in range(tops):

        @pl.loop(1, group)
        def _(step, top=top):
            term_copy(step, top, me).wait_send()
            out_copy(step, top, me).wait_send()
            out_copy(step, top, peer(step)).wait_recv()


def top_stage(sol, blocks, top_rhs, inverse, chain):
    grids, rows = lax.axis_size("grid"), lax.axis_size("row")
    group = grids * rows
    tops, size, width = top_rhs.shape
    depth = width // group
    bf16 = jnp.bfloat16
    dma = pltpu.SemaphoreType.DMA
    offset = lax.axis_index(("grid", "row")) * depth
    rhs_turned = lax.dynamic_slice_in_dim(jnp.swapaxes(top_rhs, 1, 2), offset, depth, 1)
    stacked = pl.pallas_call(
        functools.partial(top_kernel, grids, rows),
        out_shape=jax.ShapeDtypeStruct((group, tops, depth, size), bf16),
        in_specs=[VMEM, VMEM, VMEM, ANY, ANY],
        out_specs=VMEM,
        scratch_shapes=[
            pltpu.VMEM(inverse.shape, bf16),
            pltpu.VMEM(chain.shape, bf16),
            pltpu.VMEM((group, tops, depth, size), bf16),
            pltpu.VMEM((group, tops, depth, size), bf16),
            dma((2,)),
            dma((group, tops)),
            dma((group, tops)),
            dma((group, tops)),
            dma((group, tops)),
        ],
        compiler_params=pltpu.CompilerParams(
            collective_id=2, has_side_effects=True, vmem_limit_bytes=32 * 2**20
        ),
        name="top",
    )(sol, blocks, rhs_turned, inverse, chain)
    return jnp.transpose(stacked, (1, 3, 0, 2)).reshape(tops, size, width)


def shards(
    rhs_in,
    rhs_target,
    leaf_inverse,
    level_one_blocks,
    level_one_pattern,
    level_one_rhs,
    level_one_inverse,
    top_blocks,
    top_rhs,
    top_inverse,
    top_chain,
):
    device_count = lax.axis_size(("grid", "row", "col"))
    rows_local, rhs_width = rhs_in.shape
    share_rows = rows_local // device_count
    destination = rhs_target // rows_local
    ordering = jnp.argsort(destination, stable=True)
    send_rows = rhs_in[ordering].reshape(device_count, share_rows, rhs_width)
    send_places = (rhs_target % rows_local)[ordering].reshape(device_count, share_rows)
    got_rows, got_places = (
        lax.all_to_all(send_rows, ("grid", "row", "col"), split_axis=0, concat_axis=0, tiled=True),
        lax.all_to_all(
            send_places, ("grid", "row", "col"), split_axis=0, concat_axis=0, tiled=True
        ),
    )
    placed = got_rows.reshape(rows_local, rhs_width)[jnp.argsort(got_places.reshape(rows_local))]
    leaf_count, block_size = (leaf_inverse.shape[0], leaf_inverse.shape[1])
    leaf_rhs = placed.reshape(leaf_count, block_size, rhs_width)
    leaf_solution = jnp.einsum(
        "lij,ljr->lir", leaf_inverse, leaf_rhs, preferred_element_type=jnp.float32
    ).astype(jnp.bfloat16)
    solution_one = level_one(
        leaf_solution,
        level_one_blocks[0, 0, 0],
        level_one_pattern[0, 0, 0],
        level_one_rhs[0, 0],
        level_one_inverse[0, 0],
    )
    top_solution = top_stage(solution_one, top_blocks[0, 0], top_rhs, top_inverse, top_chain)
    return (leaf_solution.reshape(rows_local, rhs_width), solution_one[None, None], top_solution)


def solution(mesh):
    in_specs = (
        P(("grid", "row", "col"), None),
        P(("grid", "row", "col")),
        P(("grid", "row", "col"), None, None),
        P("grid", "row", "col", None, None, None, None),
        P("grid", "row", "col", None, None),
        P("grid", "row", None, "col"),
        P("grid", "row", None, None),
        P("grid", "row", None, None, None),
        P(None, None, "col"),
        P(),
        P(),
    )
    out_specs = (
        P(("grid", "row", "col"), None),
        P("grid", "row", None, "col"),
        P(None, None, "col"),
    )
    return jax.shard_map(shards, mesh=mesh, in_specs=in_specs, out_specs=out_specs, check_vma=False)
```

```python
import functools

import jax
import jax.numpy as jnp
from jax import lax
from jax.experimental import pallas as pl
from jax.experimental.pallas import tpu as pltpu
from jax.sharding import PartitionSpec as P

MESH = pl.DeviceIdType.MESH
VMEM = pl.BlockSpec(memory_space=pltpu.VMEM)
ANY = pl.BlockSpec(memory_space=pl.ANY)


def greet(axes, sizes):
    barrier = pltpu.get_barrier_semaphore()
    total = 1
    for size in sizes:
        total *= size
    flat = 0
    for axis, size in zip(axes, sizes):
        flat = flat * size + lax.axis_index(axis)

    @pl.loop(1, total)
    def _(step):
        rest = lax.rem(flat + step, total)
        coords = {}
        for axis, size in reversed(list(zip(axes, sizes))):
            coords[axis] = lax.rem(rest, size)
            rest = rest // size
        pl.semaphore_signal(barrier, inc=1, device_id=coords, device_id_type=MESH)

    pl.semaphore_wait(barrier, total - 1)


def dot(a, b):
    return jnp.dot(a, b, preferred_element_type=jnp.float32)


def dot_t(a, b):
    return lax.dot_general(a, b, (((1,), (1,)), ((), ())), preferred_element_type=jnp.float32)


def lower_kernel(
    sizes,
    order,
    rhs_ref,
    slot_ref,
    place_ref,
    inverse_ref,
    blocks_hbm,
    pattern_ref,
    rhs_one_ref,
    inverse_one_ref,
    leaf_ref,
    one_ref,
    perm,
    fold,
    sorted_rows,
    got,
    got_places,
    own_blocks,
    other_blocks,
    other_pattern,
    solved,
    gathered,
    totals,
    pieces,
    landed,
    load_sems,
    block_sems,
    pattern_sems,
    place_send,
    place_recv,
    row_send,
    row_recv,
    gather_send,
    gather_recv,
    piece_send,
    piece_recv,
):
    grids, rows, cols = sizes
    devices = grids * rows * cols
    row = lax.axis_index("row")
    col = lax.axis_index("col")
    me = (lax.axis_index("grid") * rows + row) * cols + col
    side = lax.rem(row, 2)
    mate = row + 1 - 2 * side
    leaves, size, _ = inverse_ref.shape
    height = leaves * size
    chunk = leaf_ref.shape[1] // cols
    half = chunk // 2
    share = got.shape[2]
    group = 128 // share

    def row_at(offset):
        pair = lax.rem(row // 2 + offset // 2, rows // 2)
        return pair * 2 + lax.rem(side + offset % 2, 2)

    def device_of(flat):
        return {
            "grid": flat // (rows * cols),
            "row": lax.rem(flat // cols, rows),
            "col": lax.rem(flat, cols),
        }

    loads = [
        pltpu.make_async_copy(blocks_hbm.at[owner], own_blocks.at[owner], load_sems.at[owner])
        for owner in range(rows)
    ]
    for load in loads:
        load.start()

    greet(("grid", "row", "col"), sizes)

    def peer(step):
        return lax.rem(me + step, devices)

    def place_copy(step, slot):
        target = peer(step)
        return pltpu.make_async_remote_copy(
            src_ref=place_ref.at[target],
            dst_ref=got_places.at[slot],
            send_sem=place_send.at[target],
            recv_sem=place_recv.at[slot],
            device_id=device_of(target),
            device_id_type=MESH,
        )

    def row_copy(part, step, slot):
        target = peer(step)
        return pltpu.make_async_remote_copy(
            src_ref=sorted_rows.at[part, target],
            dst_ref=got.at[part, slot],
            send_sem=row_send.at[part, target],
            recv_sem=row_recv.at[part, slot],
            device_id=device_of(target),
            device_id_type=MESH,
        )

    def block_copy(owner):
        return pltpu.make_async_remote_copy(
            src_ref=blocks_hbm.at[owner],
            dst_ref=other_blocks.at[owner],
            send_sem=block_sems.at[0, owner],
            recv_sem=block_sems.at[1, owner],
            device_id={"row": mate},
            device_id_type=MESH,
        )

    def gather_copy(part, target, owner):
        return pltpu.make_async_remote_copy(
            src_ref=solved.at[part, lax.rem(target, 2)],
            dst_ref=gathered.at[part, owner],
            send_sem=gather_send.at[part, target],
            recv_sem=gather_recv.at[part, owner],
            device_id={"row": target},
            device_id_type=MESH,
        )

    def piece_copy(part, which, source, from_side):
        return pltpu.make_async_remote_copy(
            src_ref=pieces.at[part, which],
            dst_ref=landed.at[source, from_side],
            send_sem=piece_send.at[part, which],
            recv_sem=piece_recv.at[source, from_side],
            device_id={"row": mate if which else row, "col": part},
            device_id_type=MESH,
        )

    pattern_copy = pltpu.make_async_remote_copy(
        src_ref=pattern_ref,
        dst_ref=other_pattern,
        send_sem=pattern_sems.at[0],
        recv_sem=pattern_sems.at[1],
        device_id={"row": mate},
        device_id_type=MESH,
    )

    @pl.loop(1, devices)
    def _(step):
        place_copy(step, me).start()

    step_rows = 256
    for begin in range(0, height, step_rows):
        index = lax.broadcasted_iota(jnp.int32, (step_rows, height), 0) + begin
        perm[begin : begin + step_rows, :] = (
            jnp.where(index == slot_ref[...], 1.0, 0.0).astype(perm.dtype)
        )
    for part in order:
        moved = dot(perm[...], rhs_ref[:, part * chunk : (part + 1) * chunk]).astype(got.dtype)
        sorted_rows[part] = moved.reshape(devices, share, chunk)

        @pl.loop(1, devices)
        def _(step, part=part):
            row_copy(part, step, me).start()

        got[part, me] = sorted_rows[part, me]
    pattern_copy.start()
    for owner in range(rows):
        block_copy(owner).start()

    got_places[me] = place_ref[me]

    @pl.loop(1, devices)
    def _(step):
        place_copy(step, peer(step)).wait_recv()

    for block in range(height // 128):
        places = got_places[block * group]
        for other in range(1, group):
            places = places + got_places[block * group + other]
        index = lax.broadcasted_iota(jnp.int32, (height, 128), 0)
        perm[:, block * 128 : (block + 1) * 128] = jnp.where(index == places, 1.0, 0.0).astype(
            perm.dtype
        )
    for leaf in range(leaves):
        span = slice(leaf * size, (leaf + 1) * size)
        fold[span, :] = dot(inverse_ref[leaf], perm[span, :]).astype(fold.dtype)

    def masked(block, mask):
        tall = block.shape[0] // mask.shape[0]
        return (block.reshape(tall, *mask.shape) * mask[None]).reshape(block.shape)

    for load in loads:
        load.wait()

    @pl.loop(0, rows)
    def _(owner):
        for leaf in range(leaves):
            own_blocks[owner, leaf] = masked(own_blocks[owner, leaf], pattern_ref[owner, leaf])

    def solve(part):
        @pl.loop(1, devices)
        def _(step):
            row_copy(part, step, peer(step)).wait_recv()

        result = dot(fold[...], got[part].reshape(height, chunk)).astype(leaf_ref.dtype)
        leaf_ref[:, part * chunk : (part + 1) * chunk] = result
        for which in range(2):
            solved[part, which] = result[:, which * half : (which + 1) * half]
        for offset in range(rows - 1, 0, -1):
            gather_copy(part, row_at(offset), row).start()
        gathered[part, row] = solved[part, side]

    def add(part, owner):
        for which, blocks in enumerate((own_blocks, other_blocks)):
            term = dot(blocks[owner, 0], gathered[part, owner, :size])
            for leaf in range(1, leaves):
                term = term + dot(
                    blocks[owner, leaf], gathered[part, owner, leaf * size : (leaf + 1) * size]
                )
            totals[which] += term

    def couple(part):
        totals[...] = jnp.zeros_like(totals)

        @pl.loop(0, rows)
        def _(offset):
            owner = row_at(offset)

            @pl.when(offset > 0)
            def _():
                gather_copy(part, owner, owner).wait_recv()

            add(part, owner)

        pieces[part] = totals[...].astype(pieces.dtype)
        piece_copy(part, 1, col, side).start()

        @pl.when(col != part)
        def _():
            piece_copy(part, 0, col, side).start()

        @pl.when(col == part)
        def _():
            landed[col, side] = pieces[part, 0]

    for at, part in enumerate(order):
        solve(part)
        if at == 0:
            pattern_copy.wait()

            @pl.loop(0, rows)
            def _(owner):
                block_copy(owner).wait()
                for leaf in range(leaves):
                    other_blocks[owner, leaf] = masked(
                        other_blocks[owner, leaf], other_pattern[owner, leaf]
                    )
        else:
            couple(order[at - 1])
    couple(order[-1])

    for step in range(cols):
        source = lax.rem(col + step, cols)
        piece_copy(0, 1, source, 1 - side).wait_recv()
        if step:
            piece_copy(0, 0, source, side).wait_recv()
    update = []
    for which in range(2):
        total = landed[0, which].astype(jnp.float32)
        for source in range(1, cols):
            total = total + landed[source, which].astype(jnp.float32)
        update.append(total)
    resid = rhs_one_ref[...].astype(jnp.float32) - jnp.concatenate(update, axis=1)
    one_ref[...] = dot(inverse_one_ref[...], resid.astype(jnp.bfloat16)).astype(one_ref.dtype)

    for part in range(cols):
        piece_copy(part, 1, col, side).wait_send()

        @pl.when(col != part)
        def _(part=part):
            piece_copy(part, 0, col, side).wait_send()

        for offset in range(1, rows):
            gather_copy(part, row_at(offset), row).wait_send()

        @pl.loop(1, devices)
        def _(step, part=part):
            row_copy(part, step, me).wait_send()

    @pl.loop(1, devices)
    def _(step):
        place_copy(step, me).wait_send()


def lower_levels(rhs_in, target, leaf_inverse, blocks, pattern, rhs, inverse):
    sizes = tuple(lax.axis_size(axis) for axis in ("grid", "row", "col"))
    grids, rows, cols = sizes
    devices = grids * rows * cols
    height, width = rhs_in.shape
    share = height // devices
    owners, leaves, size, _ = blocks.shape
    chunk = width // cols
    half = chunk // 2
    bf16 = jnp.bfloat16
    order = sorted(range(cols), key=lambda part: -abs(2 * part - (cols - 1)))

    destination = target // height
    place = target % height
    index = jnp.arange(height, dtype=jnp.int32)
    same = (destination[:, None] == destination[None, :]) & (index[:, None] < index[None, :])
    slot = destination * share + jnp.sum(same.astype(jnp.int32), axis=0)
    picked = jnp.where(slot[None, :] == index[:, None], place[None, :], 0)
    sorted_places = jnp.sum(picked, axis=1).reshape(devices, 1, share)
    group = 128 // share
    me = lax.axis_index(("grid", "row", "col"))
    lane_group = jnp.arange(128, dtype=jnp.int32) // share
    place_rows = jnp.where(
        lane_group == me % group, jnp.tile(sorted_places, (1, 1, group)), 0
    )

    mask = jnp.broadcast_to(pattern.astype(bf16)[:, :, None, None], (owners, leaves, 16, size))
    dma = pltpu.SemaphoreType.DMA
    return pl.pallas_call(
        functools.partial(lower_kernel, sizes, order),
        out_shape=(
            jax.ShapeDtypeStruct((height, width), bf16),
            jax.ShapeDtypeStruct(rhs.shape, bf16),
        ),
        in_specs=[VMEM, VMEM, VMEM, VMEM, ANY, VMEM, VMEM, VMEM],
        out_specs=(VMEM, VMEM),
        scratch_shapes=[
            pltpu.VMEM((height, height), bf16),
            pltpu.VMEM((height, height), bf16),
            pltpu.VMEM((cols, devices, share, chunk), bf16),
            pltpu.VMEM((cols, devices, share, chunk), bf16),
            pltpu.VMEM((devices, 1, 128), jnp.int32),
            pltpu.VMEM(blocks.shape, bf16),
            pltpu.VMEM(blocks.shape, bf16),
            pltpu.VMEM(mask.shape, bf16),
            pltpu.VMEM((cols, 2, height, half), bf16),
            pltpu.VMEM((cols, rows, height, half), bf16),
            pltpu.VMEM((2, size, half), jnp.float32),
            pltpu.VMEM((cols, 2, size, half), bf16),
            pltpu.VMEM((cols, 2, size, half), bf16),
            dma((rows,)),
            dma((2, rows)),
            dma((2,)),
            dma((devices,)),
            dma((devices,)),
            dma((cols, devices)),
            dma((cols, devices)),
            dma((cols, rows)),
            dma((cols, rows)),
            dma((cols, 2)),
            dma((cols, 2)),
        ],
        compiler_params=pltpu.CompilerParams(
            collective_id=1, has_side_effects=True, vmem_limit_bytes=56 * 2**20
        ),
        name="lower",
    )(rhs_in, slot[None, :], place_rows, leaf_inverse, blocks, mask, rhs, inverse)


def top_kernel(
    grids,
    rows,
    sol_ref,
    blocks_ref,
    rhs_ref,
    inverse_hbm,
    chain_hbm,
    out_ref,
    inverse_ref,
    chain_ref,
    terms,
    landed,
    load_sems,
    term_send,
    term_recv,
    out_send,
    out_recv,
):
    group = grids * rows
    me = lax.axis_index("grid") * rows + lax.axis_index("row")
    tops, size = blocks_ref.shape[0], blocks_ref.shape[1]
    depth = terms.shape[2]
    loads = (
        pltpu.make_async_copy(inverse_hbm, inverse_ref, load_sems.at[0]),
        pltpu.make_async_copy(chain_hbm, chain_ref, load_sems.at[1]),
    )
    for load in loads:
        load.start()
    greet(("grid", "row"), (grids, rows))
    turned = sol_ref[...].T

    def peer(step):
        return lax.rem(me + step, group)

    def term_copy(step, top, slot):
        target = peer(step)
        return pltpu.make_async_remote_copy(
            src_ref=terms.at[target, top],
            dst_ref=landed.at[slot, top],
            send_sem=term_send.at[target, top],
            recv_sem=term_recv.at[slot, top],
            device_id={"grid": target // rows, "row": lax.rem(target, rows)},
            device_id_type=MESH,
        )

    def out_copy(step, top, slot):
        target = peer(step)
        return pltpu.make_async_remote_copy(
            src_ref=out_ref.at[me, top],
            dst_ref=out_ref.at[slot, top],
            send_sem=out_send.at[target, top],
            recv_sem=out_recv.at[slot, top],
            device_id={"grid": target // rows, "row": lax.rem(target, rows)},
            device_id_type=MESH,
        )

    for top in range(tops):
        term = dot_t(turned, blocks_ref[top]).astype(terms.dtype)
        terms[:, top] = term.reshape(group, depth, size)

        @pl.loop(1, group)
        def _(step, top=top):
            term_copy(step, top, me).start()

    for load in loads:
        load.wait()
    for top in range(tops):

        @pl.loop(1, group)
        def _(step, top=top):
            term_copy(step, top, peer(step)).wait_recv()

        landed[me, top] = terms[me, top]
        update = landed[0, top].astype(jnp.float32)
        for other in range(1, group):
            update = update + landed[other, top].astype(jnp.float32)
        running = rhs_ref[top].astype(jnp.float32) - update
        for earlier in range(top):
            running = running - dot_t(
                out_ref[me, earlier], chain_ref[top * (top - 1) // 2 + earlier]
            )
        out_ref[me, top] = dot_t(running.astype(jnp.bfloat16), inverse_ref[top]).astype(
            jnp.bfloat16
        )

        @pl.loop(1, group)
        def _(step, top=top):
            out_copy(step, top, me).start()

    for top in range(tops):

        @pl.loop(1, group)
        def _(step, top=top):
            term_copy(step, top, me).wait_send()
            out_copy(step, top, me).wait_send()
            out_copy(step, top, peer(step)).wait_recv()


def top_stage(sol, blocks, top_rhs, inverse, chain):
    grids, rows = lax.axis_size("grid"), lax.axis_size("row")
    group = grids * rows
    tops, size, width = top_rhs.shape
    depth = width // group
    bf16 = jnp.bfloat16
    dma = pltpu.SemaphoreType.DMA
    offset = lax.axis_index(("grid", "row")) * depth
    rhs_turned = lax.dynamic_slice_in_dim(jnp.swapaxes(top_rhs, 1, 2), offset, depth, 1)
    stacked = pl.pallas_call(
        functools.partial(top_kernel, grids, rows),
        out_shape=jax.ShapeDtypeStruct((group, tops, depth, size), bf16),
        in_specs=[VMEM, VMEM, VMEM, ANY, ANY],
        out_specs=VMEM,
        scratch_shapes=[
            pltpu.VMEM(inverse.shape, bf16),
            pltpu.VMEM(chain.shape, bf16),
            pltpu.VMEM((group, tops, depth, size), bf16),
            pltpu.VMEM((group, tops, depth, size), bf16),
            dma((2,)),
            dma((group, tops)),
            dma((group, tops)),
            dma((group, tops)),
            dma((group, tops)),
        ],
        compiler_params=pltpu.CompilerParams(
            collective_id=2, has_side_effects=True, vmem_limit_bytes=32 * 2**20
        ),
        name="top",
    )(sol, blocks, rhs_turned, inverse, chain)
    return jnp.transpose(stacked, (1, 3, 0, 2)).reshape(tops, size, width)


def shards(
    rhs_in,
    rhs_target,
    leaf_inverse,
    level_one_blocks,
    level_one_pattern,
    level_one_rhs,
    level_one_inverse,
    top_blocks,
    top_rhs,
    top_inverse,
    top_chain,
):
    leaf_solution, solution_one = lower_levels(
        rhs_in,
        rhs_target,
        leaf_inverse,
        level_one_blocks[0, 0, 0],
        level_one_pattern[0, 0, 0],
        level_one_rhs[0, 0],
        level_one_inverse[0, 0],
    )
    top_solution = top_stage(solution_one, top_blocks[0, 0], top_rhs, top_inverse, top_chain)
    return (leaf_solution, solution_one[None, None], top_solution)


def solution(mesh):
    in_specs = (
        P(("grid", "row", "col"), None),
        P(("grid", "row", "col")),
        P(("grid", "row", "col"), None, None),
        P("grid", "row", "col", None, None, None, None),
        P("grid", "row", "col", None, None),
        P("grid", "row", None, "col"),
        P("grid", "row", None, None),
        P("grid", "row", None, None, None),
        P(None, None, "col"),
        P(),
        P(),
    )
    out_specs = (
        P(("grid", "row", "col"), None),
        P("grid", "row", None, "col"),
        P(None, None, "col"),
    )
    return jax.shard_map(shards, mesh=mesh, in_specs=in_specs, out_specs=out_specs, check_vma=False)
```

```python
import functools

import jax
import jax.numpy as jnp
from jax import lax
from jax.experimental import pallas as pl
from jax.experimental.pallas import tpu as pltpu
from jax.sharding import PartitionSpec as P

MESH = pl.DeviceIdType.MESH
VMEM = pl.BlockSpec(memory_space=pltpu.VMEM)
ANY = pl.BlockSpec(memory_space=pl.ANY)


def greet(axes, sizes):
    barrier = pltpu.get_barrier_semaphore()
    total = 1
    for size in sizes:
        total *= size
    flat = 0
    for axis, size in zip(axes, sizes):
        flat = flat * size + lax.axis_index(axis)

    @pl.loop(1, total)
    def _(step):
        rest = lax.rem(flat + step, total)
        coords = {}
        for axis, size in reversed(list(zip(axes, sizes))):
            coords[axis] = lax.rem(rest, size)
            rest = rest // size
        pl.semaphore_signal(barrier, inc=1, device_id=coords, device_id_type=MESH)

    return lambda: pl.semaphore_wait(barrier, total - 1)


def dot(a, b):
    return jnp.dot(a, b, preferred_element_type=jnp.float32)


def dot_t(a, b):
    return lax.dot_general(a, b, (((1,), (1,)), ((), ())), preferred_element_type=jnp.float32)


def lower_kernel(
    sizes,
    order,
    rhs_ref,
    slot_ref,
    place_ref,
    inverse_ref,
    blocks_hbm,
    pattern_ref,
    rhs_one_ref,
    inverse_one_ref,
    top_blocks_hbm,
    top_rhs_hbm,
    top_inverse_hbm,
    chain_hbm,
    leaf_ref,
    one_ref,
    top_ref,
    perm,
    fold,
    sorted_rows,
    got,
    got_places,
    own_blocks,
    other_blocks,
    other_pattern,
    solved,
    gathered,
    totals,
    pieces,
    landed,
    top_blocks,
    top_rhs,
    top_inverse,
    chain,
    rhs_turned,
    terms,
    mate_terms,
    summed,
    sums,
    load_sems,
    top_load_sems,
    block_sems,
    pattern_sems,
    place_send,
    place_recv,
    row_send,
    row_recv,
    gather_send,
    gather_recv,
    piece_send,
    piece_recv,
    mate_send,
    mate_recv,
    sum_send,
    sum_recv,
    out_send,
    out_recv,
    on_send,
    on_recv,
):
    grids, rows, cols = sizes
    devices = grids * rows * cols
    row = lax.axis_index("row")
    col = lax.axis_index("col")
    me = (lax.axis_index("grid") * rows + row) * cols + col
    side = lax.rem(row, 2)
    mate = row + 1 - 2 * side
    leaves, size, _ = inverse_ref.shape
    height = leaves * size
    chunk = leaf_ref.shape[1] // cols
    half = chunk // 2
    share = got.shape[2]
    group = 128 // share

    def row_at(offset):
        pair = lax.rem(row // 2 + offset // 2, rows // 2)
        return pair * 2 + lax.rem(side + offset % 2, 2)

    def device_of(flat):
        return {
            "grid": flat // (rows * cols),
            "row": lax.rem(flat // cols, rows),
            "col": lax.rem(flat, cols),
        }

    loads = [
        pltpu.make_async_copy(blocks_hbm.at[owner], own_blocks.at[owner], load_sems.at[owner])
        for owner in range(rows)
    ]
    met = greet(("grid", "row", "col"), sizes)
    for load in loads:
        load.start()
    top_loads = [
        pltpu.make_async_copy(source, into, top_load_sems.at[at])
        for at, (source, into) in enumerate(
            (
                (top_rhs_hbm, top_rhs),
                (top_blocks_hbm, top_blocks),
                (top_inverse_hbm, top_inverse),
                (chain_hbm, chain),
            )
        )
    ]
    for load in top_loads:
        load.start()

    def peer(step):
        return lax.rem(me + step, devices)

    def place_copy(step, slot):
        target = peer(step)
        return pltpu.make_async_remote_copy(
            src_ref=place_ref.at[target],
            dst_ref=got_places.at[slot],
            send_sem=place_send.at[target],
            recv_sem=place_recv.at[slot],
            device_id=device_of(target),
            device_id_type=MESH,
        )

    def row_copy(part, step, slot):
        target = peer(step)
        return pltpu.make_async_remote_copy(
            src_ref=sorted_rows.at[part, target],
            dst_ref=got.at[part, slot],
            send_sem=row_send.at[part, target],
            recv_sem=row_recv.at[part, slot],
            device_id=device_of(target),
            device_id_type=MESH,
        )

    def block_copy(owner):
        return pltpu.make_async_remote_copy(
            src_ref=blocks_hbm.at[owner],
            dst_ref=other_blocks.at[owner],
            send_sem=block_sems.at[0, owner],
            recv_sem=block_sems.at[1, owner],
            device_id={"row": mate},
            device_id_type=MESH,
        )

    def gather_copy(part, target, owner):
        return pltpu.make_async_remote_copy(
            src_ref=solved.at[part, lax.rem(target, 2)],
            dst_ref=gathered.at[part, owner],
            send_sem=gather_send.at[part, target],
            recv_sem=gather_recv.at[part, owner],
            device_id={"row": target},
            device_id_type=MESH,
        )

    def piece_copy(part, which, source, from_side):
        return pltpu.make_async_remote_copy(
            src_ref=pieces.at[part, which],
            dst_ref=landed.at[source, from_side],
            send_sem=piece_send.at[part, which],
            recv_sem=piece_recv.at[source, from_side],
            device_id={"row": mate if which else row, "col": part},
            device_id_type=MESH,
        )

    pattern_copy = pltpu.make_async_remote_copy(
        src_ref=pattern_ref,
        dst_ref=other_pattern,
        send_sem=pattern_sems.at[0],
        recv_sem=pattern_sems.at[1],
        device_id={"row": mate},
        device_id_type=MESH,
    )

    step_rows = 256
    for begin in range(0, height, step_rows):
        index = lax.broadcasted_iota(jnp.int32, (step_rows, height), 0) + begin
        perm[begin : begin + step_rows, :] = (
            jnp.where(index == slot_ref[...], 1.0, 0.0).astype(perm.dtype)
        )

    def send_rows(part):
        @pl.loop(1, devices)
        def _(step):
            row_copy(part, step, me).start()

    for at, part in enumerate(order):
        moved = dot(perm[...], rhs_ref[:, part * chunk : (part + 1) * chunk]).astype(got.dtype)
        sorted_rows[part] = moved.reshape(devices, share, chunk)
        if at == 0:
            met()

            @pl.loop(1, devices)
            def _(step):
                place_copy(step, me).start()

        if at < 2:
            send_rows(part)
        got[part, me] = sorted_rows[part, me]
    pattern_copy.start()
    for owner in range(rows):
        block_copy(owner).start()

    got_places[me] = place_ref[me]

    @pl.loop(1, devices)
    def _(step):
        place_copy(step, peer(step)).wait_recv()

    for block in range(height // 128):
        places = got_places[block * group]
        for other in range(1, group):
            places = places + got_places[block * group + other]
        index = lax.broadcasted_iota(jnp.int32, (height, 128), 0)
        perm[:, block * 128 : (block + 1) * 128] = jnp.where(index == places, 1.0, 0.0).astype(
            perm.dtype
        )
    for leaf in range(leaves):
        span = slice(leaf * size, (leaf + 1) * size)
        fold[span, :] = dot(inverse_ref[leaf], perm[span, :]).astype(fold.dtype)

    def masked(block, mask):
        tall = block.shape[0] // mask.shape[0]
        return (block.reshape(tall, *mask.shape) * mask[None]).reshape(block.shape)

    for load in loads + top_loads:
        load.wait()

    tops = top_blocks.shape[0]
    pairs = grids * rows // 2
    depth = terms.shape[3]
    for top in range(tops):
        rhs_turned[top] = top_rhs[top].T.reshape(2 * pairs, depth, size)

    @pl.loop(0, rows)
    def _(owner):
        for leaf in range(leaves):
            own_blocks[owner, leaf] = masked(own_blocks[owner, leaf], pattern_ref[owner, leaf])

    def solve(part):
        @pl.loop(1, devices)
        def _(step):
            row_copy(part, step, peer(step)).wait_recv()

        result = dot(fold[...], got[part].reshape(height, chunk)).astype(leaf_ref.dtype)
        leaf_ref[:, part * chunk : (part + 1) * chunk] = result
        for which in range(2):
            solved[part, which] = result[:, which * half : (which + 1) * half]
        for offset in range(rows - 1, 0, -1):
            gather_copy(part, row_at(offset), row).start()
        gathered[part, row] = solved[part, side]

    def add(part, owner):
        for which, blocks in enumerate((own_blocks, other_blocks)):
            term = dot(blocks[owner, 0], gathered[part, owner, :size])
            for leaf in range(1, leaves):
                term = term + dot(
                    blocks[owner, leaf], gathered[part, owner, leaf * size : (leaf + 1) * size]
                )
            totals[which] += term

    def couple(part):
        totals[...] = jnp.zeros_like(totals)

        @pl.loop(0, rows)
        def _(offset):
            owner = row_at(offset)

            @pl.when(offset > 0)
            def _():
                gather_copy(part, owner, owner).wait_recv()

            add(part, owner)

        pieces[part] = totals[...].astype(pieces.dtype)
        piece_copy(part, 1, col, side).start()

        @pl.when(col != part)
        def _():
            piece_copy(part, 0, col, side).start()

        @pl.when(col == part)
        def _():
            landed[col, side] = pieces[part, 0]

    for at, part in enumerate(order):
        solve(part)
        if at + 2 < cols:
            send_rows(order[at + 2])
        if at == 0:
            pattern_copy.wait()

            @pl.loop(0, rows)
            def _(owner):
                block_copy(owner).wait()
                for leaf in range(leaves):
                    other_blocks[owner, leaf] = masked(
                        other_blocks[owner, leaf], other_pattern[owner, leaf]
                    )
        else:
            couple(order[at - 1])
    couple(order[-1])

    for step in range(cols):
        source = lax.rem(col + step, cols)
        piece_copy(0, 1, source, 1 - side).wait_recv()
        if step:
            piece_copy(0, 0, source, side).wait_recv()
    update = []
    for which in range(2):
        total = landed[0, which].astype(jnp.float32)
        for source in range(1, cols):
            total = total + landed[source, which].astype(jnp.float32)
        update.append(total)
    resid = rhs_one_ref[...].astype(jnp.float32) - jnp.concatenate(update, axis=1)
    solution_one = dot(inverse_one_ref[...], resid.astype(jnp.bfloat16)).astype(one_ref.dtype)
    one_ref[...] = solution_one

    pair = (lax.axis_index("grid") * rows + row) // 2
    here = 2 * pair + side

    def pair_at(step):
        return lax.rem(pair + step, pairs)

    def across(target):
        return {
            "grid": target // (rows // 2),
            "row": lax.rem(target, rows // 2) * 2 + side,
        }

    def mate_copy(top):
        return pltpu.make_async_remote_copy(
            src_ref=terms.at[top, 1 - side],
            dst_ref=mate_terms.at[top],
            send_sem=mate_send.at[top],
            recv_sem=mate_recv.at[top],
            device_id={"row": mate},
            device_id_type=MESH,
        )

    def sum_copy(top, target, source):
        return pltpu.make_async_remote_copy(
            src_ref=summed.at[top, target],
            dst_ref=sums.at[top, source],
            send_sem=sum_send.at[top, target],
            recv_sem=sum_recv.at[top, source],
            device_id=across(target),
            device_id_type=MESH,
        )

    def out_copy(top, target, source):
        return pltpu.make_async_remote_copy(
            src_ref=top_ref.at[here, top],
            dst_ref=top_ref.at[2 * source + side, top],
            send_sem=out_send.at[top, target],
            recv_sem=out_recv.at[top, source],
            device_id=across(target),
            device_id_type=MESH,
        )

    def on_copy(top, source, from_side):
        return pltpu.make_async_remote_copy(
            src_ref=top_ref.at[2 * source + side, top],
            dst_ref=top_ref.at[2 * source + from_side, top],
            send_sem=on_send.at[top, source],
            recv_sem=on_recv.at[top, source],
            device_id={"row": mate},
            device_id_type=MESH,
        )

    turned = solution_one.T
    for top in range(tops):
        term = dot_t(turned, top_blocks[top])
        for target in range(2 * pairs):
            terms[top, target % 2, target // 2] = term[
                target * depth : (target + 1) * depth
            ].astype(terms.dtype)
        mate_copy(top).start()
    for top in range(tops):
        mate_copy(top).wait_recv()
        summed[top] = (
            terms[top, side].astype(jnp.float32) + mate_terms[top].astype(jnp.float32)
        ).astype(summed.dtype)
        for step in range(1, pairs):
            sum_copy(top, pair_at(step), pair).start()
    for top in range(tops):
        sums[top, pair] = summed[top, pair]
        for step in range(1, pairs):
            sum_copy(top, pair_at(step), pair_at(step)).wait_recv()
        update = sums[top, 0].astype(jnp.float32)
        for other in range(1, pairs):
            update = update + sums[top, other].astype(jnp.float32)
        running = rhs_turned[top, here].astype(jnp.float32) - update
        for earlier in range(top):
            running = running - dot_t(
                top_ref[here, earlier], chain[top * (top - 1) // 2 + earlier]
            )
        top_ref[here, top] = dot_t(running.astype(jnp.bfloat16), top_inverse[top]).astype(
            top_ref.dtype
        )
        for step in range(1, pairs):
            out_copy(top, pair_at(step), pair).start()
        on_copy(top, pair, side).start()
    for top in range(tops):
        for step in range(1, pairs):
            source = pair_at(step)
            out_copy(top, source, source).wait_recv()
            on_copy(top, source, side).start()
    for top in range(tops):
        for step in range(pairs):
            on_copy(top, pair_at(step), 1 - side).wait_recv()
        for step in range(pairs):
            on_copy(top, pair_at(step), side).wait_send()
            if step:
                out_copy(top, pair_at(step), pair).wait_send()
                sum_copy(top, pair_at(step), pair).wait_send()
        mate_copy(top).wait_send()

    for part in range(cols):
        piece_copy(part, 1, col, side).wait_send()

        @pl.when(col != part)
        def _(part=part):
            piece_copy(part, 0, col, side).wait_send()

        for offset in range(1, rows):
            gather_copy(part, row_at(offset), row).wait_send()

        @pl.loop(1, devices)
        def _(step, part=part):
            row_copy(part, step, me).wait_send()

    @pl.loop(1, devices)
    def _(step):
        place_copy(step, me).wait_send()


def all_levels(rhs_in, target, leaf_inverse, blocks, pattern, rhs, inverse, *top_arrays):
    sizes = tuple(lax.axis_size(axis) for axis in ("grid", "row", "col"))
    grids, rows, cols = sizes
    devices = grids * rows * cols
    height, width = rhs_in.shape
    share = height // devices
    owners, leaves, size, _ = blocks.shape
    chunk = width // cols
    half = chunk // 2
    bf16 = jnp.bfloat16
    order = sorted(range(cols), key=lambda part: -abs(2 * part - (cols - 1)))

    destination = target // height
    place = target % height
    index = jnp.arange(height, dtype=jnp.int32)
    same = (destination[:, None] == destination[None, :]) & (index[:, None] < index[None, :])
    slot = destination * share + jnp.sum(same.astype(jnp.int32), axis=0)
    picked = jnp.where(slot[None, :] == index[:, None], place[None, :], 0)
    sorted_places = jnp.sum(picked, axis=1).reshape(devices, 1, share)
    group = 128 // share
    me = lax.axis_index(("grid", "row", "col"))
    lane_group = jnp.arange(128, dtype=jnp.int32) // share
    place_rows = jnp.where(
        lane_group == me % group, jnp.tile(sorted_places, (1, 1, group)), 0
    )

    mask = jnp.broadcast_to(pattern.astype(bf16)[:, :, None, None], (owners, leaves, 16, size))
    dma = pltpu.SemaphoreType.DMA
    tops, _, top_width = top_arrays[1].shape
    pairs = grids * rows // 2
    depth = top_width // (2 * pairs)
    leaf, one, stacked = pl.pallas_call(
        functools.partial(lower_kernel, sizes, order),
        out_shape=(
            jax.ShapeDtypeStruct((height, width), bf16),
            jax.ShapeDtypeStruct(rhs.shape, bf16),
            jax.ShapeDtypeStruct((2 * pairs, tops, depth, size), bf16),
        ),
        in_specs=[VMEM, VMEM, VMEM, VMEM, ANY, VMEM, VMEM, VMEM, ANY, ANY, ANY, ANY],
        out_specs=(VMEM, VMEM, VMEM),
        scratch_shapes=[
            pltpu.VMEM((height, height), bf16),
            pltpu.VMEM((height, height), bf16),
            pltpu.VMEM((cols, devices, share, chunk), bf16),
            pltpu.VMEM((cols, devices, share, chunk), bf16),
            pltpu.VMEM((devices, 1, 128), jnp.int32),
            pltpu.VMEM(blocks.shape, bf16),
            pltpu.VMEM(blocks.shape, bf16),
            pltpu.VMEM(mask.shape, bf16),
            pltpu.VMEM((cols, 2, height, half), bf16),
            pltpu.VMEM((cols, rows, height, half), bf16),
            pltpu.VMEM((2, size, half), jnp.float32),
            pltpu.VMEM((cols, 2, size, half), bf16),
            pltpu.VMEM((cols, 2, size, half), bf16),
            *(pltpu.VMEM(array.shape, bf16) for array in top_arrays),
            pltpu.VMEM((tops, 2 * pairs, depth, size), bf16),
            pltpu.VMEM((tops, 2, pairs, depth, size), bf16),
            pltpu.VMEM((tops, pairs, depth, size), bf16),
            pltpu.VMEM((tops, pairs, depth, size), bf16),
            pltpu.VMEM((tops, pairs, depth, size), bf16),
            dma((rows,)),
            dma((len(top_arrays),)),
            dma((2, rows)),
            dma((2,)),
            dma((devices,)),
            dma((devices,)),
            dma((cols, devices)),
            dma((cols, devices)),
            dma((cols, rows)),
            dma((cols, rows)),
            dma((cols, 2)),
            dma((cols, 2)),
            dma((tops,)),
            dma((tops,)),
            *(dma((tops, pairs)) for _ in range(6)),
        ],
        compiler_params=pltpu.CompilerParams(
            collective_id=1, has_side_effects=True, vmem_limit_bytes=60 * 2**20
        ),
        name="lower",
    )(rhs_in, slot[None, :], place_rows, leaf_inverse, blocks, mask, rhs, inverse, *top_arrays)
    solved = jnp.transpose(stacked, (1, 3, 0, 2)).reshape(tops, size, top_width)
    return leaf, one, solved


def shards(
    rhs_in,
    rhs_target,
    leaf_inverse,
    level_one_blocks,
    level_one_pattern,
    level_one_rhs,
    level_one_inverse,
    top_blocks,
    top_rhs,
    top_inverse,
    top_chain,
):
    leaf_solution, solution_one, top_solution = all_levels(
        rhs_in,
        rhs_target,
        leaf_inverse,
        level_one_blocks[0, 0, 0],
        level_one_pattern[0, 0, 0],
        level_one_rhs[0, 0],
        level_one_inverse[0, 0],
        top_blocks[0, 0],
        top_rhs,
        top_inverse,
        top_chain,
    )
    return (leaf_solution, solution_one[None, None], top_solution)


def solution(mesh):
    in_specs = (
        P(("grid", "row", "col"), None),
        P(("grid", "row", "col")),
        P(("grid", "row", "col"), None, None),
        P("grid", "row", "col", None, None, None, None),
        P("grid", "row", "col", None, None),
        P("grid", "row", None, "col"),
        P("grid", "row", None, None),
        P("grid", "row", None, None, None),
        P(None, None, "col"),
        P(),
        P(),
    )
    out_specs = (
        P(("grid", "row", "col"), None),
        P("grid", "row", None, "col"),
        P(None, None, "col"),
    )
    return jax.shard_map(shards, mesh=mesh, in_specs=in_specs, out_specs=out_specs, check_vma=False)
```

```python
import functools

import jax
import jax.numpy as jnp
from jax import lax
from jax.experimental import pallas as pl
from jax.experimental.pallas import tpu as pltpu
from jax.sharding import PartitionSpec as P

MESH = pl.DeviceIdType.MESH
VMEM = pl.BlockSpec(memory_space=pltpu.VMEM)
ANY = pl.BlockSpec(memory_space=pl.ANY)


def greet(axes, sizes):
    barrier = pltpu.get_barrier_semaphore()
    total = 1
    for size in sizes:
        total *= size
    flat = 0
    for axis, size in zip(axes, sizes):
        flat = flat * size + lax.axis_index(axis)

    @pl.loop(1, total)
    def _(step):
        rest = lax.rem(flat + step, total)
        coords = {}
        for axis, size in reversed(list(zip(axes, sizes))):
            coords[axis] = lax.rem(rest, size)
            rest = rest // size
        pl.semaphore_signal(barrier, inc=1, device_id=coords, device_id_type=MESH)

    return lambda: pl.semaphore_wait(barrier, total - 1)


def dot(a, b):
    return jnp.dot(a, b, preferred_element_type=jnp.float32)


def dot_t(a, b):
    return lax.dot_general(a, b, (((1,), (1,)), ((), ())), preferred_element_type=jnp.float32)


def lower_kernel(
    sizes,
    order,
    rhs_ref,
    slot_ref,
    place_ref,
    inverse_ref,
    blocks_hbm,
    pattern_ref,
    rhs_one_ref,
    inverse_one_ref,
    top_blocks_hbm,
    top_rhs_hbm,
    top_inverse_hbm,
    chain_hbm,
    leaf_ref,
    one_ref,
    turned_ref,
    perm,
    fold,
    sorted_rows,
    got,
    got_places,
    own_blocks,
    other_blocks,
    other_pattern,
    solved,
    gathered,
    totals,
    pieces,
    landed,
    top_blocks,
    top_rhs,
    top_inverse,
    chain,
    rhs_turned,
    terms,
    mate_terms,
    summed,
    sums,
    top_ref,
    load_sems,
    top_load_sems,
    block_sems,
    pattern_sems,
    place_send,
    place_recv,
    row_send,
    row_recv,
    gather_send,
    gather_recv,
    piece_send,
    piece_recv,
    mate_send,
    mate_recv,
    sum_send,
    sum_recv,
    out_send,
    out_recv,
    on_send,
    on_recv,
):
    grids, rows, cols = sizes
    devices = grids * rows * cols
    row = lax.axis_index("row")
    col = lax.axis_index("col")
    me = (lax.axis_index("grid") * rows + row) * cols + col
    side = lax.rem(row, 2)
    mate = row + 1 - 2 * side
    leaves, size, _ = inverse_ref.shape
    height = leaves * size
    chunk = leaf_ref.shape[1] // cols
    half = chunk // 2
    share = got.shape[2]
    group = 128 // share

    def row_at(offset):
        pair = lax.rem(row // 2 + offset // 2, rows // 2)
        return pair * 2 + lax.rem(side + offset % 2, 2)

    def device_of(flat):
        return {
            "grid": flat // (rows * cols),
            "row": lax.rem(flat // cols, rows),
            "col": lax.rem(flat, cols),
        }

    loads = [
        pltpu.make_async_copy(blocks_hbm.at[owner], own_blocks.at[owner], load_sems.at[owner])
        for owner in range(rows)
    ]
    met = greet(("grid", "row", "col"), sizes)
    for load in loads:
        load.start()
    top_loads = [
        pltpu.make_async_copy(source, into, top_load_sems.at[at])
        for at, (source, into) in enumerate(
            (
                (top_rhs_hbm, top_rhs),
                (top_blocks_hbm, top_blocks),
                (top_inverse_hbm, top_inverse),
                (chain_hbm, chain),
            )
        )
    ]
    for load in top_loads:
        load.start()

    def peer(step):
        return lax.rem(me + step, devices)

    def place_copy(step, slot):
        target = peer(step)
        return pltpu.make_async_remote_copy(
            src_ref=place_ref.at[target],
            dst_ref=got_places.at[slot],
            send_sem=place_send.at[target],
            recv_sem=place_recv.at[slot],
            device_id=device_of(target),
            device_id_type=MESH,
        )

    def row_copy(part, step, slot):
        target = peer(step)
        return pltpu.make_async_remote_copy(
            src_ref=sorted_rows.at[part, target],
            dst_ref=got.at[part, slot],
            send_sem=row_send.at[part, target],
            recv_sem=row_recv.at[part, slot],
            device_id=device_of(target),
            device_id_type=MESH,
        )

    def block_copy(owner):
        return pltpu.make_async_remote_copy(
            src_ref=blocks_hbm.at[owner],
            dst_ref=other_blocks.at[owner],
            send_sem=block_sems.at[0, owner],
            recv_sem=block_sems.at[1, owner],
            device_id={"row": mate},
            device_id_type=MESH,
        )

    def gather_copy(part, target, owner):
        return pltpu.make_async_remote_copy(
            src_ref=solved.at[part, lax.rem(target, 2)],
            dst_ref=gathered.at[part, owner],
            send_sem=gather_send.at[part, target],
            recv_sem=gather_recv.at[part, owner],
            device_id={"row": target},
            device_id_type=MESH,
        )

    def piece_copy(part, which, source, from_side):
        return pltpu.make_async_remote_copy(
            src_ref=pieces.at[part, which],
            dst_ref=landed.at[source, from_side],
            send_sem=piece_send.at[part, which],
            recv_sem=piece_recv.at[source, from_side],
            device_id={"row": mate if which else row, "col": part},
            device_id_type=MESH,
        )

    pattern_copy = pltpu.make_async_remote_copy(
        src_ref=pattern_ref,
        dst_ref=other_pattern,
        send_sem=pattern_sems.at[0],
        recv_sem=pattern_sems.at[1],
        device_id={"row": mate},
        device_id_type=MESH,
    )

    step_rows = 256
    for begin in range(0, height, step_rows):
        index = lax.broadcasted_iota(jnp.int32, (step_rows, height), 0) + begin
        perm[begin : begin + step_rows, :] = (
            jnp.where(index == slot_ref[...], 1.0, 0.0).astype(perm.dtype)
        )

    def send_rows(part):
        @pl.loop(1, devices)
        def _(step):
            row_copy(part, step, me).start()

    for at, part in enumerate(order):
        moved = dot(perm[...], rhs_ref[:, part * chunk : (part + 1) * chunk]).astype(got.dtype)
        sorted_rows[part] = moved.reshape(devices, share, chunk)
        if at == 0:
            met()

            @pl.loop(1, devices)
            def _(step):
                place_copy(step, me).start()

        if at < 2:
            send_rows(part)
        got[part, me] = sorted_rows[part, me]
    pattern_copy.start()
    for owner in range(rows):
        block_copy(owner).start()

    got_places[me] = place_ref[me]

    @pl.loop(1, devices)
    def _(step):
        place_copy(step, peer(step)).wait_recv()

    for block in range(height // 128):
        places = got_places[block * group]
        for other in range(1, group):
            places = places + got_places[block * group + other]
        index = lax.broadcasted_iota(jnp.int32, (height, 128), 0)
        perm[:, block * 128 : (block + 1) * 128] = jnp.where(index == places, 1.0, 0.0).astype(
            perm.dtype
        )
    for leaf in range(leaves):
        span = slice(leaf * size, (leaf + 1) * size)
        fold[span, :] = dot(inverse_ref[leaf], perm[span, :]).astype(fold.dtype)

    def masked(block, mask):
        tall = block.shape[0] // mask.shape[0]
        return (block.reshape(tall, *mask.shape) * mask[None]).reshape(block.shape)

    for load in loads + top_loads:
        load.wait()

    tops = top_blocks.shape[0]
    pairs = grids * rows // 2
    depth = terms.shape[3]
    for top in range(tops):
        rhs_turned[top] = top_rhs[top].T.reshape(2 * pairs, depth, size)

    @pl.loop(0, rows)
    def _(owner):
        for leaf in range(leaves):
            own_blocks[owner, leaf] = masked(own_blocks[owner, leaf], pattern_ref[owner, leaf])

    def solve(part):
        @pl.loop(1, devices)
        def _(step):
            row_copy(part, step, peer(step)).wait_recv()

        result = dot(fold[...], got[part].reshape(height, chunk)).astype(leaf_ref.dtype)
        leaf_ref[:, part * chunk : (part + 1) * chunk] = result
        for which in range(2):
            solved[part, which] = result[:, which * half : (which + 1) * half]
        for offset in range(rows - 1, 0, -1):
            gather_copy(part, row_at(offset), row).start()
        gathered[part, row] = solved[part, side]

    def add(part, owner):
        for which, blocks in enumerate((own_blocks, other_blocks)):
            term = dot(blocks[owner, 0], gathered[part, owner, :size])
            for leaf in range(1, leaves):
                term = term + dot(
                    blocks[owner, leaf], gathered[part, owner, leaf * size : (leaf + 1) * size]
                )
            totals[which] += term

    def couple(part):
        totals[...] = jnp.zeros_like(totals)

        @pl.loop(0, rows)
        def _(offset):
            owner = row_at(offset)

            @pl.when(offset > 0)
            def _():
                gather_copy(part, owner, owner).wait_recv()

            add(part, owner)

        pieces[part] = totals[...].astype(pieces.dtype)
        piece_copy(part, 1, col, side).start()

        @pl.when(col != part)
        def _():
            piece_copy(part, 0, col, side).start()

        @pl.when(col == part)
        def _():
            landed[col, side] = pieces[part, 0]

    for at, part in enumerate(order):
        solve(part)
        if at + 2 < cols:
            send_rows(order[at + 2])
        if at == 0:
            pattern_copy.wait()

            @pl.loop(0, rows)
            def _(owner):
                block_copy(owner).wait()
                for leaf in range(leaves):
                    other_blocks[owner, leaf] = masked(
                        other_blocks[owner, leaf], other_pattern[owner, leaf]
                    )
        else:
            couple(order[at - 1])
    couple(order[-1])

    for step in range(cols):
        source = lax.rem(col + step, cols)
        piece_copy(0, 1, source, 1 - side).wait_recv()
        if step:
            piece_copy(0, 0, source, side).wait_recv()
    update = []
    for which in range(2):
        total = landed[0, which].astype(jnp.float32)
        for source in range(1, cols):
            total = total + landed[source, which].astype(jnp.float32)
        update.append(total)
    resid = rhs_one_ref[...].astype(jnp.float32) - jnp.concatenate(update, axis=1)
    solution_one = dot(inverse_one_ref[...], resid.astype(jnp.bfloat16)).astype(one_ref.dtype)
    one_ref[...] = solution_one

    pair = (lax.axis_index("grid") * rows + row) // 2
    here = 2 * pair + side

    def pair_at(step):
        return lax.rem(pair + step, pairs)

    def across(target):
        return {
            "grid": target // (rows // 2),
            "row": lax.rem(target, rows // 2) * 2 + side,
        }

    def mate_copy(top):
        return pltpu.make_async_remote_copy(
            src_ref=terms.at[top, 1 - side],
            dst_ref=mate_terms.at[top],
            send_sem=mate_send.at[top],
            recv_sem=mate_recv.at[top],
            device_id={"row": mate},
            device_id_type=MESH,
        )

    def sum_copy(top, target, source):
        return pltpu.make_async_remote_copy(
            src_ref=summed.at[top, target],
            dst_ref=sums.at[top, source],
            send_sem=sum_send.at[top, target],
            recv_sem=sum_recv.at[top, source],
            device_id=across(target),
            device_id_type=MESH,
        )

    def out_copy(top, target, source):
        return pltpu.make_async_remote_copy(
            src_ref=top_ref.at[here, top],
            dst_ref=top_ref.at[2 * source + side, top],
            send_sem=out_send.at[top, target],
            recv_sem=out_recv.at[top, source],
            device_id=across(target),
            device_id_type=MESH,
        )

    def on_copy(top, source, from_side):
        return pltpu.make_async_remote_copy(
            src_ref=top_ref.at[2 * source + side, top],
            dst_ref=top_ref.at[2 * source + from_side, top],
            send_sem=on_send.at[top, source],
            recv_sem=on_recv.at[top, source],
            device_id={"row": mate},
            device_id_type=MESH,
        )

    turned = solution_one.T
    for top in range(tops):
        term = dot_t(turned, top_blocks[top])
        for target in range(2 * pairs):
            terms[top, target % 2, target // 2] = term[
                target * depth : (target + 1) * depth
            ].astype(terms.dtype)
        mate_copy(top).start()
    for top in range(tops):
        mate_copy(top).wait_recv()
        summed[top] = (
            terms[top, side].astype(jnp.float32) + mate_terms[top].astype(jnp.float32)
        ).astype(summed.dtype)
        for step in range(1, pairs):
            sum_copy(top, pair_at(step), pair).start()
    for top in range(tops):
        sums[top, pair] = summed[top, pair]
        for step in range(1, pairs):
            sum_copy(top, pair_at(step), pair_at(step)).wait_recv()
        update = sums[top, 0].astype(jnp.float32)
        for other in range(1, pairs):
            update = update + sums[top, other].astype(jnp.float32)
        running = rhs_turned[top, here].astype(jnp.float32) - update
        for earlier in range(top):
            running = running - dot_t(
                top_ref[here, earlier], chain[top * (top - 1) // 2 + earlier]
            )
        top_ref[here, top] = dot_t(running.astype(jnp.bfloat16), top_inverse[top]).astype(
            top_ref.dtype
        )
        for step in range(1, pairs):
            out_copy(top, pair_at(step), pair).start()
        on_copy(top, pair, side).start()
    for top in range(tops):
        for step in range(1, pairs):
            source = pair_at(step)
            out_copy(top, source, source).wait_recv()
            on_copy(top, source, side).start()
    for top in range(tops):
        for step in range(pairs):
            on_copy(top, pair_at(step), 1 - side).wait_recv()
        turned_ref[top] = top_ref[:, top].reshape(2 * pairs * depth, size).T
    for top in range(tops):
        for step in range(pairs):
            on_copy(top, pair_at(step), side).wait_send()
            if step:
                out_copy(top, pair_at(step), pair).wait_send()
                sum_copy(top, pair_at(step), pair).wait_send()
        mate_copy(top).wait_send()

    for part in range(cols):
        piece_copy(part, 1, col, side).wait_send()

        @pl.when(col != part)
        def _(part=part):
            piece_copy(part, 0, col, side).wait_send()

        for offset in range(1, rows):
            gather_copy(part, row_at(offset), row).wait_send()

        @pl.loop(1, devices)
        def _(step, part=part):
            row_copy(part, step, me).wait_send()

    @pl.loop(1, devices)
    def _(step):
        place_copy(step, me).wait_send()


def all_levels(rhs_in, target, leaf_inverse, blocks, pattern, rhs, inverse, *top_arrays):
    sizes = tuple(lax.axis_size(axis) for axis in ("grid", "row", "col"))
    grids, rows, cols = sizes
    devices = grids * rows * cols
    height, width = rhs_in.shape
    share = height // devices
    owners, leaves, size, _ = blocks.shape
    chunk = width // cols
    half = chunk // 2
    bf16 = jnp.bfloat16
    order = sorted(range(cols), key=lambda part: -abs(2 * part - (cols - 1)))

    destination = lax.div(target, jnp.int32(height))
    place = lax.rem(target, jnp.int32(height))
    index = jnp.arange(height, dtype=jnp.int32)
    same = (destination[:, None] == destination[None, :]) & (index[:, None] < index[None, :])
    slot = destination * share + jnp.sum(same.astype(jnp.int32), axis=0)
    picked = jnp.where(slot[None, :] == index[:, None], place[None, :], 0)
    sorted_places = jnp.sum(picked, axis=1).reshape(devices, 1, share)
    group = 128 // share
    me = lax.axis_index(("grid", "row", "col"))
    lane_group = jnp.arange(128, dtype=jnp.int32) // share
    place_rows = jnp.where(
        lane_group == me % group, jnp.tile(sorted_places, (1, 1, group)), 0
    )

    mask = jnp.broadcast_to(pattern.astype(bf16)[:, :, None, None], (owners, leaves, 16, size))
    dma = pltpu.SemaphoreType.DMA
    tops, _, top_width = top_arrays[1].shape
    pairs = grids * rows // 2
    depth = top_width // (2 * pairs)
    return pl.pallas_call(
        functools.partial(lower_kernel, sizes, order),
        out_shape=(
            jax.ShapeDtypeStruct((height, width), bf16),
            jax.ShapeDtypeStruct(rhs.shape, bf16),
            jax.ShapeDtypeStruct((tops, size, top_width), bf16),
        ),
        in_specs=[VMEM, VMEM, VMEM, VMEM, ANY, VMEM, VMEM, VMEM, ANY, ANY, ANY, ANY],
        out_specs=(VMEM, VMEM, VMEM),
        scratch_shapes=[
            pltpu.VMEM((height, height), bf16),
            pltpu.VMEM((height, height), bf16),
            pltpu.VMEM((cols, devices, share, chunk), bf16),
            pltpu.VMEM((cols, devices, share, chunk), bf16),
            pltpu.VMEM((devices, 1, 128), jnp.int32),
            pltpu.VMEM(blocks.shape, bf16),
            pltpu.VMEM(blocks.shape, bf16),
            pltpu.VMEM(mask.shape, bf16),
            pltpu.VMEM((cols, 2, height, half), bf16),
            pltpu.VMEM((cols, rows, height, half), bf16),
            pltpu.VMEM((2, size, half), jnp.float32),
            pltpu.VMEM((cols, 2, size, half), bf16),
            pltpu.VMEM((cols, 2, size, half), bf16),
            *(pltpu.VMEM(array.shape, bf16) for array in top_arrays),
            pltpu.VMEM((tops, 2 * pairs, depth, size), bf16),
            pltpu.VMEM((tops, 2, pairs, depth, size), bf16),
            pltpu.VMEM((tops, pairs, depth, size), bf16),
            pltpu.VMEM((tops, pairs, depth, size), bf16),
            pltpu.VMEM((tops, pairs, depth, size), bf16),
            pltpu.VMEM((2 * pairs, tops, depth, size), bf16),
            dma((rows,)),
            dma((len(top_arrays),)),
            dma((2, rows)),
            dma((2,)),
            dma((devices,)),
            dma((devices,)),
            dma((cols, devices)),
            dma((cols, devices)),
            dma((cols, rows)),
            dma((cols, rows)),
            dma((cols, 2)),
            dma((cols, 2)),
            dma((tops,)),
            dma((tops,)),
            *(dma((tops, pairs)) for _ in range(6)),
        ],
        compiler_params=pltpu.CompilerParams(
            collective_id=1, has_side_effects=True, vmem_limit_bytes=60 * 2**20
        ),
        name="lower",
    )(rhs_in, slot[None, :], place_rows, leaf_inverse, blocks, mask, rhs, inverse, *top_arrays)


def shards(
    rhs_in,
    rhs_target,
    leaf_inverse,
    level_one_blocks,
    level_one_pattern,
    level_one_rhs,
    level_one_inverse,
    top_blocks,
    top_rhs,
    top_inverse,
    top_chain,
):
    leaf_solution, solution_one, top_solution = all_levels(
        rhs_in,
        rhs_target,
        leaf_inverse,
        level_one_blocks[0, 0, 0],
        level_one_pattern[0, 0, 0],
        level_one_rhs[0, 0],
        level_one_inverse[0, 0],
        top_blocks[0, 0],
        top_rhs,
        top_inverse,
        top_chain,
    )
    return (leaf_solution, solution_one[None, None], top_solution)


def solution(mesh):
    in_specs = (
        P(("grid", "row", "col"), None),
        P(("grid", "row", "col")),
        P(("grid", "row", "col"), None, None),
        P("grid", "row", "col", None, None, None, None),
        P("grid", "row", "col", None, None),
        P("grid", "row", None, "col"),
        P("grid", "row", None, None),
        P("grid", "row", None, None, None),
        P(None, None, "col"),
        P(),
        P(),
    )
    out_specs = (
        P(("grid", "row", "col"), None),
        P("grid", "row", None, "col"),
        P(None, None, "col"),
    )
    return jax.shard_map(shards, mesh=mesh, in_specs=in_specs, out_specs=out_specs, check_vma=False)
```
